512 devices in a mesh: dp: 32 (over y, x, core), fsdp: 16 (over z).
Axes of the slice: x: 4, y: 4, z: 16, core: 2. Of those that a mesh axis runs over, the one named last changes fastest.
Arguments:
- queries: bfloat16 [131072, 2048], P(('dp', 'fsdp')), may hold values from -600 to 600
- w_kv: bfloat16 [2, 2048, 896], P(None, 'fsdp'), may hold values from -0.1875 to 0.1875
- encodings: bfloat16 [196608, 896], P(('dp', 'fsdp')), may hold values from -6 to 6
- counts: int32 [512], P(('dp', 'fsdp')), may hold values from 48 to 384, as said below
- owner_rank: int32 [196608], P(('dp', 'fsdp')), may hold values from 0 to 31, as said below
- owner_span: int32 [196608], P(('dp', 'fsdp')), may hold values from 0 to 3, as said below
- grad_ctx: bfloat16 [131072, 2048], P(('dp', 'fsdp')), may hold values from -24 to 24
Outputs:
- grad_queries: bfloat16 [131072, 2048], P(('dp', 'fsdp'))
- grad_value: bfloat16 [2048, 896], P('fsdp')
The draws below stay inside these ranges and needn't reach their ends.
Inputs may be any that keep to these rules, and one draw needn't show every extreme that they name: `counts`: each count is 384 divided by 1, 2, 4 or 8; among the devices of equal fsdp index one holds 384. `owner_rank`: among the live rows of one device at most 12 name the same owner; a device whose count is 384 names every owner exactly 12 times. `owner_span`: every span of every decoder device is named by at least one live row of a device with equal fsdp index.
All inputs are finite; a program needn't handle non-finite values.
Results may differ from the reference program's by a relative error of at most 0.023.
Values may be sent and summed in bfloat16 or wider, within the bound.
No kernel may reach another device: no remote copies, remote signals or barrier semaphores. Data moves between devices by JAX's collectives and lax.ppermute only.
A program may use at most 64 MiB of HBM per device.

```python
import jax
import jax.numpy as jnp
from jax import lax

HEADS = 16
HEAD_DIM = 128
ENC = 896
SPAN = 64
TOK_DEV = 256
ENC_ROWS_DEV = 384
HW = 2048
SPANS_DEV = 4
PAIR_CAP = 12
TOKENS = 131072
ENC_ROWS = 196608
N_DP = 32
N_FSDP = 16
DEVICES = 512


def routing_tables(key):
    base = jax.random.fold_in(key, 11)
    key_shift, key_full, key_order, key_offset = jax.random.split(base, 4)
    shifts = jax.random.randint(key_shift, (N_DP, N_FSDP), 0, 4)
    full_index = jax.random.randint(key_full, (N_FSDP,), 0, N_DP)
    shifts = jnp.where(jnp.arange(N_DP)[:, None] == full_index[None, :], 0, shifts)
    live_counts = jnp.right_shift(jnp.full((N_DP, N_FSDP), ENC_ROWS_DEV, jnp.int32), shifts.astype(jnp.int32))
    order_scores = jax.random.randint(key_order, (DEVICES, ENC_ROWS_DEV), 0, 4096) * ENC_ROWS_DEV + jnp.arange(ENC_ROWS_DEV)[None, :]
    ordering = jnp.argsort(order_scores, axis=1, stable=True).astype(jnp.int32)
    offsets = jax.random.randint(key_offset, (DEVICES, 1), 0, SPANS_DEV)
    ranks = (ordering // PAIR_CAP).reshape(-1).astype(jnp.int32)
    spans = ((ordering + offsets) % SPANS_DEV).reshape(-1).astype(jnp.int32)
    return (live_counts.reshape(-1).astype(jnp.int32), ranks, spans)


def draw_counts(key, part):
    return routing_tables(key)[0]


def draw_owner_rank(key, part):
    return routing_tables(key)[1]


def draw_owner_span(key, part):
    return routing_tables(key)[2]


def draw_queries(key, part):
    base = jax.random.fold_in(key, 3)
    key_main = jax.random.fold_in(base, 0)
    values = jnp.clip(jax.random.normal(key_main, (TOKENS, HW), jnp.float32), -6.0, 6.0)
    return values.astype(jnp.bfloat16)


def raised(values, stream_key, source, target, parts, factor):
    owner, partner = [(jnp.arange(values.shape[dim]) // (values.shape[dim] // parts)).reshape([-1 if axis == dim else 1 for axis in range(values.ndim)]) for dim in (source, target)]
    chosen = jax.random.permutation(stream_key, parts)[partner]
    strong = (owner == chosen) | (owner == (partner + parts // 2) % parts)
    return jnp.where(strong, factor * values, values)


def steps_of(key, extent, cuts, least, top_value):
    gain, own = 1.0, jax.random.fold_in(key, 6)
    for position, parts in cuts:
        draws = jnp.exp(jax.random.uniform(jax.random.fold_in(own, position), (parts,), jnp.float32, least / len(cuts), top_value / len(cuts)))
        gain = gain * jnp.repeat(draws, extent[position] // parts).reshape([-1 if axis == position else 1 for axis in range(len(extent))])
    return gain


def gaussian(stream_key, shape, deviation, limit, pieces=(), kind=jnp.bfloat16):
    drawn = jax.random.normal(stream_key, shape, jnp.float32) * deviation
    if len(pieces) > 0:
        drawn = steps_of(stream_key, shape, pieces, -0.22, 0.18) * drawn
    return jnp.clip(drawn, min=-limit, max=limit).astype(kind)


def heavy_noise(rng, shape, deviation, reach, cuts, heavy, kind=jnp.bfloat16):
    array = deviation * jax.random.normal(rng, shape, jnp.float32)
    if cuts:
        array = array * steps_of(rng, shape, cuts, -0.22, 0.18)
    return jnp.clip(raised(array, jax.random.fold_in(rng, 3), *heavy), -reach, reach).astype(kind)


def setup_inputs(seed: int = 0) -> dict:
    key_list = jax.random.split(jax.random.key(seed), 8)
    queries = draw_queries(jax.random.fold_in(key_list[7], 71), 0)
    w_kv = gaussian(key_list[1], (2, HW, ENC), ENC ** -0.5, 0.1875, ((1, 16),))
    encodings = gaussian(key_list[2], (ENC_ROWS, ENC), 1.0, 6.0, ((0, 512),))
    counts = draw_counts(jax.random.fold_in(key_list[7], 71), 0)
    owner_rank = draw_owner_rank(jax.random.fold_in(key_list[7], 71), 0)
    owner_span = draw_owner_span(jax.random.fold_in(key_list[7], 71), 0)
    grad_ctx = heavy_noise(key_list[6], (TOKENS, HW), 1.0, 24.0, ((0, 512),), (0, 1, 512, 6.0))
    return dict(queries=queries, w_kv=w_kv, encodings=encodings, counts=counts, owner_rank=owner_rank, owner_span=owner_span, grad_ctx=grad_ctx)


def pack_rows(enc_rows, live_count, rank_rows, span_rows):
    row_total = enc_rows.shape[0]
    pair_slots = row_total // N_DP
    live_rows = jnp.arange(row_total, dtype=jnp.int32) < live_count
    hit_table = ((rank_rows[:, None] == jnp.arange(N_DP, dtype=jnp.int32)[None, :]) & live_rows[:, None]).astype(jnp.int32)
    before_hits = jnp.cumsum(hit_table, axis=0) - hit_table
    slot_index = jnp.sum(before_hits * hit_table, axis=1)
    target = jnp.where(live_rows, rank_rows * pair_slots + slot_index, N_DP * pair_slots).astype(jnp.int32)
    buffer = jnp.zeros((N_DP * pair_slots, enc_rows.shape[1]), enc_rows.dtype).at[target].set(enc_rows, mode="drop")
    tag_buffer = jnp.full((N_DP * pair_slots,), -1, jnp.int32).at[target].set(span_rows, mode="drop")
    return buffer.reshape(N_DP, pair_slots, enc_rows.shape[1]), tag_buffer.reshape(N_DP, pair_slots)


def device_step(total, inputs, w_kv):
    query_rows, cotangent, received, tag_rows = inputs
    contract = (((1,), (1,)), ((), ()))
    keys = lax.dot_general(received, w_kv[0], contract, preferred_element_type=jnp.float32).astype(jnp.bfloat16)
    values = lax.dot_general(received, w_kv[1], contract, preferred_element_type=jnp.float32).astype(jnp.bfloat16)
    token_total = query_rows.shape[0]
    slot_total = received.shape[0]
    scale = 1.0 / (HEAD_DIM ** 0.5)
    query_heads = query_rows.reshape(token_total, HEADS, HEAD_DIM).astype(jnp.float32)
    key_heads = keys.reshape(slot_total, HEADS, HEAD_DIM).astype(jnp.float32)
    value_heads = values.reshape(slot_total, HEADS, HEAD_DIM).astype(jnp.float32)
    grad_heads = cotangent.reshape(token_total, HEADS, HEAD_DIM).astype(jnp.float32)
    scores = jnp.einsum("thd,khd->htk", query_heads, key_heads) * scale
    token_span = jnp.arange(token_total, dtype=jnp.int32) // SPAN
    allowed = (token_span[:, None] == tag_rows[None, :])[None]
    masked = jnp.where(allowed, scores, -1e30)
    highest = jnp.max(masked, axis=-1, keepdims=True)
    weights = jnp.where(allowed, jnp.exp(masked - highest), 0.0)
    probs = weights / jnp.sum(weights, axis=-1, keepdims=True)
    probs_low = probs.astype(jnp.bfloat16)
    context = jnp.einsum("htk,khd->thd", probs_low.astype(jnp.float32), value_heads)
    dprob = jnp.einsum("thd,khd->htk", grad_heads, value_heads)
    delta = jnp.transpose(jnp.sum(grad_heads * context, axis=-1))[:, :, None]
    dscore = (probs * (dprob - delta)).astype(jnp.bfloat16)
    grad_query = (jnp.einsum("htk,khd->thd", dscore.astype(jnp.float32), key_heads) * scale).astype(jnp.bfloat16)
    dval = jnp.einsum("htk,thd->khd", probs_low.astype(jnp.float32), grad_heads).astype(jnp.bfloat16)
    dval = dval.reshape(slot_total, HW)
    partial_value = lax.dot_general(dval, received, (((0,), (0,)), ((), ())), preferred_element_type=jnp.float32)
    total = total + partial_value.astype(jnp.bfloat16).astype(jnp.float32)
    return total, grad_query.reshape(token_total, HW)


def reference(queries, w_kv, encodings, counts, owner_rank, owner_span, grad_ctx):
    device_total = N_DP * N_FSDP
    enc_blocks = encodings.reshape(N_DP, N_FSDP, ENC_ROWS_DEV, ENC)
    count_blocks = counts.reshape(N_DP, N_FSDP)
    rank_blocks = owner_rank.reshape(N_DP, N_FSDP, ENC_ROWS_DEV)
    span_blocks = owner_span.reshape(N_DP, N_FSDP, ENC_ROWS_DEV)
    packer = jax.vmap(jax.vmap(pack_rows))
    sent, sent_tags = packer(enc_blocks, count_blocks, rank_blocks, span_blocks)
    received = jnp.transpose(sent, (2, 1, 0, 3, 4)).reshape(device_total, ENC_ROWS_DEV, ENC)
    tags = jnp.transpose(sent_tags, (2, 1, 0, 3)).reshape(device_total, ENC_ROWS_DEV)
    query_blocks = queries.reshape(device_total, TOK_DEV, HW)
    grad_blocks = grad_ctx.reshape(device_total, TOK_DEV, HW)
    start_total = jnp.zeros((HW, ENC), jnp.float32)
    final_total, grad_queries = lax.scan(partial_fn(w_kv), start_total, (query_blocks, grad_blocks, received, tags))
    grad_value = (final_total / N_DP).astype(jnp.bfloat16)
    return grad_queries.reshape(TOKENS, HW), grad_value


def partial_fn(w_kv):
    def stepper(total, inputs):
        return device_step(total, inputs, w_kv)
    return stepper
```

```python
import jax
import jax.numpy as jnp
from jax import lax
from jax.experimental import pallas as pl
from jax.experimental.pallas import tpu as pltpu
from jax.sharding import Mesh
from jax.sharding import PartitionSpec as P

HEADS = 16
HEAD_DIM = 128
SPAN = 64
ENC = 896
TOK = 256
ROWS = 384
DP = 32
CAP = 12
PLANE = 16
HALF = HEADS // 2
EXT = ENC + 128
BIG = 2.0**100
SCALE = 1.0 / HEAD_DIM**0.5
LOG2E = 1.4426950408889634


NN = (((1,), (0,)), ((), ()))
NT = (((1,), (1,)), ((), ()))
TN = (((0,), (0,)), ((), ()))


def dot(a, b, dims):
    return lax.dot_general(a, b, dims, preferred_element_type=jnp.float32)


def pack_body(count_ref, rank_ref, span_ref, enc_ref, out_ref):
    rank = rank_ref[...]
    live = lax.broadcasted_iota(jnp.int32, (1, ROWS), 1) < count_ref[0]
    owner = lax.broadcasted_iota(jnp.int32, (DP, ROWS), 0)
    hit = ((owner == rank) & live).astype(jnp.float32)
    earlier = lax.broadcasted_iota(jnp.int32, (ROWS, ROWS), 0) < lax.broadcasted_iota(jnp.int32, (ROWS, ROWS), 1)
    before = dot(hit.astype(jnp.bfloat16), earlier.astype(jnp.float32).astype(jnp.bfloat16), NN)
    slot = jnp.sum(before * hit, axis=0, keepdims=True).astype(jnp.int32)
    target = jnp.where(live, rank * CAP + slot, -1)
    place = (lax.broadcasted_iota(jnp.int32, (ROWS, ROWS), 0) == target).astype(jnp.float32).astype(jnp.bfloat16)
    spans = (lax.broadcasted_iota(jnp.int32, (128, ROWS), 0) == span_ref[...]).astype(jnp.float32).astype(jnp.bfloat16)
    out_ref[:, :ENC] = dot(place, enc_ref[...], NN).astype(jnp.bfloat16)
    out_ref[:, ENC:] = dot(place, spans, NT).astype(jnp.bfloat16)


def pack(counts, rank, span, enc, interpret=False):
    vmem = pl.BlockSpec(memory_space=pltpu.VMEM)
    return pl.pallas_call(
        pack_body,
        out_shape=jax.ShapeDtypeStruct((ROWS, EXT), jnp.bfloat16),
        in_specs=[pl.BlockSpec(memory_space=pltpu.SMEM), vmem, vmem, vmem],
        out_specs=vmem,
        interpret=interpret,
        name="pack",
    )(counts, rank.reshape(1, ROWS), span.reshape(1, ROWS), enc)


def attend_body(
    core_ref, own_ref, other_ref, q_ref, g_ref, q2_ref, g2_ref, wk_ref, wv_ref,
    gq_ref, gq2_ref, part_ref, rows_ref, mask_ref,
):
    core = core_ref[0]

    @pl.when(pl.program_id(0) == 0)
    def _():
        row = lax.broadcasted_iota(jnp.int32, (ROWS, ROWS), 0)
        col = lax.broadcasted_iota(jnp.int32, (ROWS, ROWS), 1)
        second = row // (ROWS // 2)
        rest = row - second * (ROWS // 2)
        chip = rest // CAP
        place = jnp.where(core == 0, second, 1 - second)
        source = chip * (2 * CAP) + place * CAP + (rest - chip * CAP)
        select = (source == col).astype(jnp.float32).astype(jnp.bfloat16)
        lane = lax.broadcasted_iota(jnp.int32, (ROWS // 2, 128), 1)
        for k, ref in enumerate((own_ref, other_ref)):
            moved = dot(select, ref[...], NN)
            for p in range(2):
                part = moved[p * (ROWS // 2) : (p + 1) * (ROWS // 2)]
                at = pl.ds(p * ROWS + k * (ROWS // 2), ROWS // 2)
                rows_ref[at, :] = part[:, :ENC].astype(jnp.bfloat16)
                mask_ref[at, :] = jnp.where(lane < 4, (part[:, ENC:] - 1.0) * BIG, 0.0).astype(jnp.bfloat16)

    rows = rows_ref[...]
    keys = dot(rows, wk_ref[...].reshape(HEAD_DIM, ENC), NT).astype(jnp.bfloat16)
    values = dot(rows, wv_ref[...].reshape(HEAD_DIM, ENC), NT).astype(jnp.bfloat16)
    token = lax.broadcasted_iota(jnp.int32, (TOK, 128), 0)
    spans = (lax.broadcasted_iota(jnp.int32, (TOK, 128), 1) == token // SPAN).astype(jnp.float32).astype(jnp.bfloat16)
    dvals = []
    own = (q_ref[...], g_ref[...], gq_ref)
    sibling = (q2_ref[...].reshape(TOK, HEAD_DIM), g2_ref[...].reshape(TOK, HEAD_DIM), gq2_ref)
    for k, (q, g, out_ref) in enumerate((own, sibling)):
        at = slice(k * ROWS, (k + 1) * ROWS)
        key, value, mask = keys[at], values[at], mask_ref[at, :]
        scores = dot(jnp.concatenate([q, spans], 1), jnp.concatenate([key, mask], 1), NT)
        highest = jnp.max(scores, axis=1, keepdims=True)
        weights = jnp.exp2((scores - highest) * (SCALE * LOG2E))
        probs = weights * (1.0 / jnp.sum(weights, axis=1, keepdims=True))
        low = probs.astype(jnp.bfloat16)
        dprob = dot(g, value, NT)
        delta = jnp.sum(low.astype(jnp.float32) * dprob, axis=1, keepdims=True)
        dscore = (probs * (dprob - delta)).astype(jnp.bfloat16)
        out_ref[...] = (dot(dscore, key, NN) * SCALE).astype(jnp.bfloat16)
        dvals.append(dot(g, low, TN).astype(jnp.bfloat16))
    partial = dot(jnp.concatenate(dvals, 1), rows, NN)
    part_ref[...] = partial.reshape(PLANE, 1, 8, ENC).astype(jnp.bfloat16)


def attend(core, own, other, q, g, qg2, weights, interpret=False):
    half_tokens = HALF * HEAD_DIM
    whole = lambda shape: pl.BlockSpec(shape, lambda h, c: (0,) * len(shape))
    mine = pl.BlockSpec((TOK, HEAD_DIM), lambda h, c: (0, c[0] * HALF + h))
    kv = lambda pick: pl.BlockSpec((PLANE, 1, 1, 8, ENC), lambda h, c: (0, pick(c[0]), h, 0, 0))
    return pl.pallas_call(
        attend_body,
        grid_spec=pltpu.PrefetchScalarGridSpec(
            num_scalar_prefetch=1,
            grid=(HALF,),
            in_specs=[
                whole((ROWS, EXT)),
                whole((ROWS, EXT)),
                mine,
                mine,
                pl.BlockSpec((1, TOK, HEAD_DIM), lambda h, c: (0, 0, h)),
                pl.BlockSpec((1, TOK, HEAD_DIM), lambda h, c: (1, 0, h)),
                kv(lambda c: c),
                kv(lambda c: 1 - c),
            ],
            out_specs=[
                mine,
                pl.BlockSpec((TOK, HEAD_DIM), lambda h, c: (0, h)),
                pl.BlockSpec((PLANE, 1, 8, ENC), lambda h, c: (0, h, 0, 0)),
            ],
            scratch_shapes=[
                pltpu.VMEM((2 * ROWS, ENC), jnp.bfloat16),
                pltpu.VMEM((2 * ROWS, 128), jnp.bfloat16),
            ],
        ),
        out_shape=[
            jax.ShapeDtypeStruct((TOK, HEADS * HEAD_DIM), jnp.bfloat16),
            jax.ShapeDtypeStruct((TOK, half_tokens), jnp.bfloat16),
            jax.ShapeDtypeStruct((PLANE, HALF, 8, ENC), jnp.bfloat16),
        ],
        interpret=interpret,
        name="attend",
    )(core, own, other, q, g, qg2, qg2, weights, weights)


def swap(array):
    return lax.ppermute(array, "c", [(0, 1), (1, 0)])


def exchange(array, axis):
    return lax.all_to_all(array, axis, split_axis=0, concat_axis=0, tiled=True)


def spread(array, axis, count):
    return exchange(jnp.broadcast_to(array[None], (count,) + array.shape), axis)


def total(array):
    return array.astype(jnp.float32).sum(0)


def local(queries, w_kv, encodings, counts, owner_rank, owner_span, grad_ctx):
    c = lax.axis_index("c")
    plane = lax.axis_index("y") * 4 + lax.axis_index("x")
    piece = lax.dynamic_slice(w_kv, (c, plane * 8, 0), (1, 8, ENC))[0]
    heads = spread(piece, "z", HEADS)
    kept = lax.dynamic_slice(heads, (c * HALF, 0, 0), (HALF, 8, ENC))
    given = lax.dynamic_slice(heads, ((1 - c) * HALF, 0, 0), (HALF, 8, ENC))
    mine = jnp.stack([kept, swap(given)])

    half = HALF * HEAD_DIM
    qg2 = swap(
        jnp.stack([lax.dynamic_slice(a, (0, (1 - c) * half), (TOK, half)) for a in (queries, grad_ctx)])
    )
    packed = pack(counts, owner_rank, owner_span, encodings)
    arrived = exchange(packed.reshape(PLANE, 2 * CAP, EXT), ("y", "x")).reshape(ROWS, EXT)
    other = swap(arrived)
    weights = spread(mine, ("y", "x"), PLANE)

    core = c.astype(jnp.int32).reshape(1)
    gq, gq2, part = attend(core, arrived, other, queries, grad_ctx, qg2, weights)
    grad_queries = lax.dynamic_update_slice(gq, swap(gq2), (0, (1 - c) * half))

    plane_sum = total(exchange(part, ("y", "x"))).astype(jnp.bfloat16)
    pieces = exchange(jnp.concatenate([plane_sum, plane_sum]), "z")
    final = (total(pieces) / DP).astype(jnp.bfloat16)
    block = spread(final, ("y", "x"), PLANE).reshape(HEAD_DIM, ENC)
    grad_value = jnp.where(lax.axis_index("z") // HALF == c, block, swap(block))
    return grad_queries, grad_value


def solution(mesh):
    fine = Mesh(mesh.devices.reshape(4, 4, 2, HEADS), ("y", "x", "c", "z"))
    every = ("y", "x", "c", "z")
    in_specs = (
        P(every, None),
        P(None, "z", None),
        P(every, None),
        P(every),
        P(every),
        P(every),
        P(every, None),
    )
    out_specs = (P(every, None), P("z", None))
    return jax.shard_map(local, mesh=fine, in_specs=in_specs, out_specs=out_specs, check_vma=False)
```

```python
import jax
import jax.numpy as jnp
from jax import lax
from jax.experimental import pallas as pl
from jax.experimental.pallas import tpu as pltpu
from jax.sharding import Mesh
from jax.sharding import PartitionSpec as P

HEADS = 16
HEAD_DIM = 128
SPAN = 64
ENC = 896
TOK = 256
ROWS = 384
DP = 32
CAP = 12
PLANE = 16
HALF = HEADS // 2
GROUP = HALF // 2
EXT = ENC + 128
BIG = 2.0**100
SCALE = 1.0 / HEAD_DIM**0.5
LOG2E = 1.4426950408889634


NN = (((1,), (0,)), ((), ()))
NT = (((1,), (1,)), ((), ()))
TN = (((0,), (0,)), ((), ()))


def dot(a, b, dims):
    return lax.dot_general(a, b, dims, preferred_element_type=jnp.float32)


def pack_body(count_ref, rank_ref, span_ref, enc_ref, out_ref):
    rank = rank_ref[...]
    live = lax.broadcasted_iota(jnp.int32, (1, ROWS), 1) < count_ref[0]
    owner = lax.broadcasted_iota(jnp.int32, (DP, ROWS), 0)
    hit = ((owner == rank) & live).astype(jnp.float32)
    earlier = lax.broadcasted_iota(jnp.int32, (ROWS, ROWS), 0) < lax.broadcasted_iota(jnp.int32, (ROWS, ROWS), 1)
    before = dot(hit.astype(jnp.bfloat16), earlier.astype(jnp.float32).astype(jnp.bfloat16), NN)
    slot = jnp.sum(before * hit, axis=0, keepdims=True).astype(jnp.int32)
    target = jnp.where(live, rank * CAP + slot, -1)
    place = (lax.broadcasted_iota(jnp.int32, (ROWS, ROWS), 0) == target).astype(jnp.float32).astype(jnp.bfloat16)
    spans = (lax.broadcasted_iota(jnp.int32, (128, ROWS), 0) == span_ref[...]).astype(jnp.float32).astype(jnp.bfloat16)
    out_ref[:, :ENC] = dot(place, enc_ref[...], NN).astype(jnp.bfloat16)
    out_ref[:, ENC:] = dot(place, spans, NT).astype(jnp.bfloat16)


def pack(counts, rank, span, enc, interpret=False):
    vmem = pl.BlockSpec(memory_space=pltpu.VMEM)
    return pl.pallas_call(
        pack_body,
        out_shape=jax.ShapeDtypeStruct((ROWS, EXT), jnp.bfloat16),
        in_specs=[pl.BlockSpec(memory_space=pltpu.SMEM), vmem, vmem, vmem],
        out_specs=vmem,
        interpret=interpret,
        name="pack",
    )(counts, rank.reshape(1, ROWS), span.reshape(1, ROWS), enc)


def choose(i, options):
    result = options[-1]
    for k in range(len(options) - 2, -1, -1):
        result = jnp.where(i == k, options[k], result)
    return result


def head_of(i, place, offsets):
    even, odd = offsets
    turn = jnp.where((place[0] + place[1]) % 2 == 0, choose(i, even), choose(i, odd))
    return (place[1] + turn + HEADS) % HEADS


NEAR = ((2, -2, 4, 0), (1, -1, 3, -3))
FAR = ((-4, 6, -6, 8), (5, -5, 7, -7))


def attend_step(rows_ref, mask_ref, q_ref, g_ref, q2_ref, g2_ref, w_ref, gq_ref, gq2_ref, part_ref, dval_ref):
    step = pl.program_id(0)
    rows = rows_ref[...]
    pair = dot(rows, w_ref[...], NT).astype(jnp.bfloat16)
    token = lax.broadcasted_iota(jnp.int32, (TOK, 128), 0)
    spans = (lax.broadcasted_iota(jnp.int32, (TOK, 128), 1) == token // SPAN).astype(jnp.float32).astype(jnp.bfloat16)
    for k, (q, g, out_ref) in enumerate(((q_ref, g_ref, gq_ref), (q2_ref, g2_ref, gq2_ref))):
        at = slice(k * ROWS, (k + 1) * ROWS)
        key, value = pair[at, :HEAD_DIM], pair[at, HEAD_DIM:]
        scores = dot(jnp.concatenate([q[...], spans], 1), jnp.concatenate([key, mask_ref[at, :]], 1), NT)
        highest = jnp.max(scores, axis=1, keepdims=True)
        weights = jnp.exp2((scores - highest) * (SCALE * LOG2E))
        probs = weights * (1.0 / jnp.sum(weights, axis=1, keepdims=True))
        low = probs.astype(jnp.bfloat16)
        dprob = dot(g[...], value, NT)
        delta = jnp.sum(low.astype(jnp.float32) * dprob, axis=1, keepdims=True)
        dscore = (probs * (dprob - delta)).astype(jnp.bfloat16)
        out_ref[...] = (dot(dscore, key, NN) * SCALE).astype(jnp.bfloat16)
        turned = dot(g[...], low, TN).astype(jnp.bfloat16)
        dval_ref[pl.ds(pl.multiple_of(step * HEAD_DIM, HEAD_DIM), HEAD_DIM), at] = turned

    @pl.when(step == GROUP - 1)
    def _():
        partial = dot(dval_ref[...], rows, NN)
        for j in range(GROUP):
            block = partial[j * HEAD_DIM : (j + 1) * HEAD_DIM]
            part_ref[:, j, :, :] = block.reshape(PLANE, 8, ENC).astype(jnp.bfloat16)


def near_body(
    place_ref, own_ref, other_ref, q_ref, g_ref, q2_ref, g2_ref, w0_ref, w1_ref, w2_ref, w3_ref,
    gq_ref, gq2_ref, part_ref, rows_ref, mask_ref, w_ref, dval_ref,
):
    step = pl.program_id(0)

    @pl.when(step == 0)
    def _():
        row = lax.broadcasted_iota(jnp.int32, (ROWS, ROWS), 0)
        col = lax.broadcasted_iota(jnp.int32, (ROWS, ROWS), 1)
        second = row // (ROWS // 2)
        rest = row - second * (ROWS // 2)
        chip = rest // CAP
        owner = jnp.where(place_ref[0] == 0, second, 1 - second)
        source = chip * (2 * CAP) + owner * CAP + (rest - chip * CAP)
        select = (source == col).astype(jnp.float32).astype(jnp.bfloat16)
        lane = lax.broadcasted_iota(jnp.int32, (ROWS // 2, 128), 1)
        for k, ref in enumerate((own_ref, other_ref)):
            moved = dot(select, ref[...], NN)
            for p in range(2):
                part = moved[p * (ROWS // 2) : (p + 1) * (ROWS // 2)]
                at = pl.ds(p * ROWS + k * (ROWS // 2), ROWS // 2)
                rows_ref[at, :] = part[:, :ENC].astype(jnp.bfloat16)
                mask_ref[at, :] = jnp.where(lane < 4, (part[:, ENC:] - 1.0) * BIG, 0.0).astype(jnp.bfloat16)

    for j, ref in enumerate((w0_ref, w1_ref, w2_ref, w3_ref)):

        @pl.when(step == j)
        def _(ref=ref):
            w_ref[...] = ref[...].reshape(2 * HEAD_DIM, ENC)

    attend_step(rows_ref, mask_ref, q_ref, g_ref, q2_ref, g2_ref, w_ref, gq_ref, gq2_ref, part_ref, dval_ref)


def far_body(
    place_ref, rows_ref, mask_ref, q_ref, g_ref, q2_ref, g2_ref, wk_ref, wv_ref, a0, a1, a2,
    gq_ref, gq2_ref, part_ref, w_ref, dval_ref,
):
    w_ref[:HEAD_DIM, :] = wk_ref[...].reshape(HEAD_DIM, ENC)
    w_ref[HEAD_DIM:, :] = wv_ref[...].reshape(HEAD_DIM, ENC)
    attend_step(rows_ref, mask_ref, q_ref, g_ref, q2_ref, g2_ref, w_ref, gq_ref, gq2_ref, part_ref, dval_ref)


WIDE = jax.ShapeDtypeStruct((TOK, HEADS * HEAD_DIM), jnp.bfloat16)
PART = jax.ShapeDtypeStruct((PLANE, HALF, 8, ENC), jnp.bfloat16)


def whole(*shape):
    return pl.BlockSpec(shape, lambda i, place: (0,) * len(shape))


def head_block(offsets):
    return pl.BlockSpec((TOK, HEAD_DIM), lambda i, place: (0, head_of(i, place, offsets)))


def part_block(group):
    return pl.BlockSpec((PLANE, GROUP, 8, ENC), lambda i, place: (0, group, 0, 0))


WORK = [pltpu.VMEM((2 * HEAD_DIM, ENC), jnp.bfloat16), pltpu.VMEM((GROUP * HEAD_DIM, 2 * ROWS), jnp.bfloat16)]


def attend_near(place, own, other, tokens, weights, interpret=False):
    head = head_block(NEAR)
    return pl.pallas_call(
        near_body,
        grid_spec=pltpu.PrefetchScalarGridSpec(
            num_scalar_prefetch=1,
            grid=(GROUP,),
            in_specs=[whole(ROWS, EXT)] * 2 + [head] * 4 + [whole(2, HEAD_DIM, ENC)] * 4,
            out_specs=[head, head, part_block(0), whole(2 * ROWS, ENC), whole(2 * ROWS, 128)],
            scratch_shapes=WORK,
        ),
        out_shape=[
            WIDE,
            WIDE,
            PART,
            jax.ShapeDtypeStruct((2 * ROWS, ENC), jnp.bfloat16),
            jax.ShapeDtypeStruct((2 * ROWS, 128), jnp.bfloat16),
        ],
        interpret=interpret,
        name="near",
    )(place, own, other, *tokens, *weights)


def attend_far(place, rows, mask, tokens, weights, gq, gq2, part, interpret=False):
    head = head_block(FAR)
    kv = lambda pick: pl.BlockSpec((PLANE, 1, 1, 8, ENC), lambda i, place: (0, pick(place[0]), i, 0, 0))
    kept = pl.BlockSpec(memory_space=pl.ANY)
    return pl.pallas_call(
        far_body,
        grid_spec=pltpu.PrefetchScalarGridSpec(
            num_scalar_prefetch=1,
            grid=(GROUP,),
            in_specs=[whole(2 * ROWS, ENC), whole(2 * ROWS, 128)]
            + [head] * 4
            + [kv(lambda c: c), kv(lambda c: 1 - c)]
            + [kept] * 3,
            out_specs=[head, head, part_block(1)],
            scratch_shapes=WORK,
        ),
        out_shape=[WIDE, WIDE, PART],
        input_output_aliases={9: 0, 10: 1, 11: 2},
        interpret=interpret,
        name="far",
    )(place, rows, mask, *tokens, weights, weights, gq, gq2, part)


def deal_body(place_ref, mine_ref, theirs_ref, kept_ref, given_ref):
    kept_ref[...] = mine_ref[...]
    given_ref[...] = theirs_ref[...]


def deal(place, heads, interpret=False):
    row = lambda index: pl.BlockSpec((1, 8, ENC), index)
    out = row(lambda i, place: (i, 0, 0))
    shape = jax.ShapeDtypeStruct((GROUP, 8, ENC), jnp.bfloat16)
    return pl.pallas_call(
        deal_body,
        grid_spec=pltpu.PrefetchScalarGridSpec(
            num_scalar_prefetch=1,
            grid=(GROUP,),
            in_specs=[
                row(lambda i, place: (head_of(i, place, FAR), 0, 0)),
                row(lambda i, place: (head_of(i, place, FAR[::-1]), 0, 0)),
            ],
            out_specs=[out, out],
        ),
        out_shape=[shape, shape],
        interpret=interpret,
        name="deal",
    )(place, heads, heads)


def gather_body(place_ref, part_ref, out_ref):
    out_ref[...] = jnp.sum(part_ref[...].astype(jnp.float32), axis=0).astype(jnp.bfloat16)


def gather(place, part, interpret=False):
    both = tuple(n + f for n, f in zip(NEAR, FAR))
    return pl.pallas_call(
        gather_body,
        grid_spec=pltpu.PrefetchScalarGridSpec(
            num_scalar_prefetch=1,
            grid=(HALF,),
            in_specs=[pl.BlockSpec((PLANE, 1, 8, ENC), lambda i, place: (0, i, 0, 0))],
            out_specs=pl.BlockSpec((1, 8, ENC), lambda i, place: (head_of(i, place, both), 0, 0)),
        ),
        out_shape=jax.ShapeDtypeStruct((HEADS, 8, ENC), jnp.bfloat16),
        interpret=interpret,
        name="gather",
    )(place, part)


def swap(array):
    return lax.ppermute(array, "c", [(0, 1), (1, 0)])


def exchange(array, axis):
    return lax.all_to_all(array, axis, split_axis=0, concat_axis=0, tiled=True)


def spread(array, axis, count):
    return exchange(jnp.broadcast_to(array[None], (count,) + array.shape), axis)


def total(array):
    return array.astype(jnp.float32).sum(0)


def fetch(array, even, odd):
    pairs = []
    for c in range(2):
        for z in range(HEADS):
            turn = odd if (c + z) % 2 else even
            core = 1 - c if (turn % 2 == 0) == (even != 0) else c
            pairs.append((core * HEADS + (z + turn) % HEADS, c * HEADS + z))
    assert len({a for a, _ in pairs}) == len(pairs)
    return lax.ppermute(array, ("c", "z"), pairs)


def local(queries, w_kv, encodings, counts, owner_rank, owner_span, grad_ctx):
    c = lax.axis_index("c")
    z = lax.axis_index("z")
    place = jnp.stack([c, z]).astype(jnp.int32)
    plane = lax.axis_index("y") * 4 + lax.axis_index("x")
    piece = lax.dynamic_slice(w_kv, (c, plane * 8, 0), (1, 8, ENC))[0]
    heads = spread(piece, "z", HEADS)
    kept, given = deal(place, heads)
    mine = jnp.stack([kept, swap(given)])
    near = [fetch(w_kv, even, odd) for even, odd in zip(*NEAR)]

    packed = pack(counts, owner_rank, owner_span, encodings)
    arrived = exchange(packed.reshape(PLANE, 2 * CAP, EXT), ("y", "x")).reshape(ROWS, EXT)
    other = swap(arrived)
    weights = spread(mine, ("y", "x"), PLANE)
    tokens = (queries, grad_ctx, swap(queries), swap(grad_ctx))

    gq, gq2, part, rows, mask = attend_near(place, arrived, other, tokens, near)
    gq, gq2, part = attend_far(place, rows, mask, tokens, weights, gq, gq2, part)

    sums = gather(place, exchange(part, ("y", "x")))
    final = (total(exchange(sums, "z")) / DP).astype(jnp.bfloat16)
    block = spread(final, ("y", "x"), PLANE).reshape(HEAD_DIM, ENC)
    grad_value = jnp.where(z % 2 == c, block, swap(block))
    own_head = (lax.broadcasted_iota(jnp.int32, gq.shape, 1) // HEAD_DIM) % 2 == c
    return jnp.where(own_head, gq, swap(gq2)), grad_value


def solution(mesh):
    fine = Mesh(mesh.devices.reshape(4, 4, 2, HEADS), ("y", "x", "c", "z"))
    every = ("y", "x", "c", "z")
    in_specs = (
        P(every, None),
        P(None, "z", None),
        P(every, None),
        P(every),
        P(every),
        P(every),
        P(every, None),
    )
    out_specs = (P(every, None), P("z", None))
    return jax.shard_map(local, mesh=fine, in_specs=in_specs, out_specs=out_specs, check_vma=False)
```

```python
import jax
import jax.numpy as jnp
from jax import lax
from jax.experimental import pallas as pl
from jax.experimental.pallas import tpu as pltpu
from jax.sharding import Mesh
from jax.sharding import PartitionSpec as P

HEADS = 16
HEAD_DIM = 128
SPAN = 64
ENC = 896
TOK = 256
ROWS = 384
DP = 32
CAP = 12
PLANE = 16
EXT = ENC + 128
BIG = 2.0**100
SCALE = 1.0 / HEAD_DIM**0.5
LOG2E = 1.4426950408889634


NN = (((1,), (0,)), ((), ()))
NT = (((1,), (1,)), ((), ()))
TN = (((0,), (0,)), ((), ()))


def dot(a, b, dims):
    return lax.dot_general(a, b, dims, preferred_element_type=jnp.float32)


def pack_body(count_ref, rank_ref, span_ref, enc_ref, out_ref):
    rank = rank_ref[...]
    live = lax.broadcasted_iota(jnp.int32, (1, ROWS), 1) < count_ref[0]
    owner = lax.broadcasted_iota(jnp.int32, (DP, ROWS), 0)
    hit = ((owner == rank) & live).astype(jnp.float32)
    earlier = lax.broadcasted_iota(jnp.int32, (ROWS, ROWS), 0) < lax.broadcasted_iota(jnp.int32, (ROWS, ROWS), 1)
    before = dot(hit.astype(jnp.bfloat16), earlier.astype(jnp.float32).astype(jnp.bfloat16), NN)
    slot = jnp.sum(before * hit, axis=0, keepdims=True).astype(jnp.int32)
    target = jnp.where(live, rank * CAP + slot, -1)
    place = (lax.broadcasted_iota(jnp.int32, (ROWS, ROWS), 0) == target).astype(jnp.float32).astype(jnp.bfloat16)
    spans = (lax.broadcasted_iota(jnp.int32, (128, ROWS), 0) == span_ref[...]).astype(jnp.float32).astype(jnp.bfloat16)
    out_ref[:, :ENC] = dot(place, enc_ref[...], NN).astype(jnp.bfloat16)
    out_ref[:, ENC:] = dot(place, spans, NT).astype(jnp.bfloat16)


def pack(counts, rank, span, enc, interpret=False):
    vmem = pl.BlockSpec(memory_space=pltpu.VMEM)
    return pl.pallas_call(
        pack_body,
        out_shape=jax.ShapeDtypeStruct((ROWS, EXT), jnp.bfloat16),
        in_specs=[pl.BlockSpec(memory_space=pltpu.SMEM), vmem, vmem, vmem],
        out_specs=vmem,
        interpret=interpret,
        name="pack",
    )(counts, rank.reshape(1, ROWS), span.reshape(1, ROWS), enc)


NEAR = ((2, -2, 0), (1, -1, 3), (1, -1, -3))
FAR = ((4, -4, 6, -6, 8), (-3, 5, -5, 7, -7), (3, 5, -5, 7, -7))


def choose(i, options):
    if isinstance(i, int):
        return options[i]
    result = options[-1]
    for k in range(len(options) - 2, -1, -1):
        result = jnp.where(i == k, options[k], result)
    return result


def head_of(i, c, z, offsets):
    even, first, second = (choose(i, row) for row in offsets)
    turn = jnp.where((c + z) % 2 == 0, even, jnp.where(c == 0, first, second))
    return (z + turn + HEADS) % HEADS


def attend_step(rows_ref, mask_ref, q_ref, g_ref, q2_ref, g2_ref, w_ref, gq_ref, gq2_ref, part_ref, dval_ref):
    step = pl.program_id(0)
    group = part_ref.shape[1]
    rows = rows_ref[...]
    pair = dot(rows, w_ref[...], NT).astype(jnp.bfloat16)
    token = lax.broadcasted_iota(jnp.int32, (TOK, 128), 0)
    spans = (lax.broadcasted_iota(jnp.int32, (TOK, 128), 1) == token // SPAN).astype(jnp.float32).astype(jnp.bfloat16)
    for k, (q, g, out_ref) in enumerate(((q_ref, g_ref, gq_ref), (q2_ref, g2_ref, gq2_ref))):
        at = slice(k * ROWS, (k + 1) * ROWS)
        key, value = pair[at, :HEAD_DIM], pair[at, HEAD_DIM:]
        scores = dot(jnp.concatenate([q[...], spans], 1), jnp.concatenate([key, mask_ref[at, :]], 1), NT)
        highest = jnp.max(scores, axis=1, keepdims=True)
        weights = jnp.exp2((scores - highest) * (SCALE * LOG2E))
        probs = weights * (1.0 / jnp.sum(weights, axis=1, keepdims=True))
        low = probs.astype(jnp.bfloat16)
        dprob = dot(g[...], value, NT)
        delta = jnp.sum(low.astype(jnp.float32) * dprob, axis=1, keepdims=True)
        dscore = (probs * (dprob - delta)).astype(jnp.bfloat16)
        out_ref[...] = (dot(dscore, key, NN) * SCALE).astype(jnp.bfloat16)
        turned = dot(g[...], low, TN).astype(jnp.bfloat16)
        dval_ref[pl.ds(pl.multiple_of(step * HEAD_DIM, HEAD_DIM), HEAD_DIM), at] = turned

    @pl.when(step == group - 1)
    def _():
        partial = dot(dval_ref[...], rows, NN)
        for j in range(group):
            block = partial[j * HEAD_DIM : (j + 1) * HEAD_DIM]
            part_ref[:, j, :, :] = block.reshape(PLANE, 8, ENC).astype(jnp.bfloat16)


def near_body(
    place_ref, own_ref, other_ref, q_ref, g_ref, q2_ref, g2_ref, w0_ref, w1_ref, w2_ref,
    gq_ref, gq2_ref, part_ref, rows_ref, mask_ref, w_ref, dval_ref,
):
    step = pl.program_id(0)

    @pl.when(step == 0)
    def _():
        row = lax.broadcasted_iota(jnp.int32, (ROWS, ROWS), 0)
        col = lax.broadcasted_iota(jnp.int32, (ROWS, ROWS), 1)
        second = row // (ROWS // 2)
        rest = row - second * (ROWS // 2)
        chip = rest // CAP
        owner = jnp.where(place_ref[0] == 0, second, 1 - second)
        source = chip * (2 * CAP) + owner * CAP + (rest - chip * CAP)
        select = (source == col).astype(jnp.float32).astype(jnp.bfloat16)
        lane = lax.broadcasted_iota(jnp.int32, (ROWS // 2, 128), 1)
        for k, ref in enumerate((own_ref, other_ref)):
            moved = dot(select, ref[...], NN)
            for p in range(2):
                part = moved[p * (ROWS // 2) : (p + 1) * (ROWS // 2)]
                at = pl.ds(p * ROWS + k * (ROWS // 2), ROWS // 2)
                rows_ref[at, :] = part[:, :ENC].astype(jnp.bfloat16)
                mask_ref[at, :] = jnp.where(lane < 4, (part[:, ENC:] - 1.0) * BIG, 0.0).astype(jnp.bfloat16)

    for j, ref in enumerate((w0_ref, w1_ref, w2_ref)):

        @pl.when(step == j)
        def _(ref=ref):
            w_ref[...] = ref[...].reshape(2 * HEAD_DIM, ENC)

    attend_step(rows_ref, mask_ref, q_ref, g_ref, q2_ref, g2_ref, w_ref, gq_ref, gq2_ref, part_ref, dval_ref)


def far_body(
    place_ref, rows_ref, mask_ref, q_ref, g_ref, q2_ref, g2_ref, wk_ref, wv_ref, a0, a1,
    gq_ref, gq2_ref, part_ref, w_ref, dval_ref,
):
    w_ref[:HEAD_DIM, :] = wk_ref[...].reshape(HEAD_DIM, ENC)
    w_ref[HEAD_DIM:, :] = wv_ref[...].reshape(HEAD_DIM, ENC)
    attend_step(rows_ref, mask_ref, q_ref, g_ref, q2_ref, g2_ref, w_ref, gq_ref, gq2_ref, part_ref, dval_ref)


WIDE = jax.ShapeDtypeStruct((TOK, HEADS * HEAD_DIM), jnp.bfloat16)


def whole(*shape):
    return pl.BlockSpec(shape, lambda i, place: (0,) * len(shape))


def head_block(offsets):
    return pl.BlockSpec((TOK, HEAD_DIM), lambda i, place: (0, head_of(i, place[0], place[1], offsets)))


def part_of(group):
    return jax.ShapeDtypeStruct((PLANE, group, 8, ENC), jnp.bfloat16)


def work(group):
    return [pltpu.VMEM((2 * HEAD_DIM, ENC), jnp.bfloat16), pltpu.VMEM((group * HEAD_DIM, 2 * ROWS), jnp.bfloat16)]


def attend_near(place, own, other, tokens, weights, interpret=False):
    head = head_block(NEAR)
    group = len(weights)
    return pl.pallas_call(
        near_body,
        grid_spec=pltpu.PrefetchScalarGridSpec(
            num_scalar_prefetch=1,
            grid=(group,),
            in_specs=[whole(ROWS, EXT)] * 2 + [head] * 4 + [whole(2, HEAD_DIM, ENC)] * group,
            out_specs=[head, head, whole(PLANE, group, 8, ENC), whole(2 * ROWS, ENC), whole(2 * ROWS, 128)],
            scratch_shapes=work(group),
        ),
        out_shape=[
            WIDE,
            WIDE,
            part_of(group),
            jax.ShapeDtypeStruct((2 * ROWS, ENC), jnp.bfloat16),
            jax.ShapeDtypeStruct((2 * ROWS, 128), jnp.bfloat16),
        ],
        interpret=interpret,
        name="near",
    )(place, own, other, *tokens, *weights)


def attend_far(place, rows, mask, tokens, weights, gq, gq2, interpret=False):
    head = head_block(FAR)
    group = weights.shape[2]
    kv = lambda pick: pl.BlockSpec((PLANE, 1, 1, 8, ENC), lambda i, place: (0, pick(place[0]), i, 0, 0))
    kept = pl.BlockSpec(memory_space=pl.ANY)
    return pl.pallas_call(
        far_body,
        grid_spec=pltpu.PrefetchScalarGridSpec(
            num_scalar_prefetch=1,
            grid=(group,),
            in_specs=[whole(2 * ROWS, ENC), whole(2 * ROWS, 128)]
            + [head] * 4
            + [kv(lambda c: c), kv(lambda c: 1 - c)]
            + [kept] * 2,
            out_specs=[head, head, whole(PLANE, group, 8, ENC)],
            scratch_shapes=work(group),
        ),
        out_shape=[WIDE, WIDE, part_of(group)],
        input_output_aliases={9: 0, 10: 1},
        interpret=interpret,
        name="far",
    )(place, rows, mask, *tokens, weights, weights, gq, gq2)


def deal_body(place_ref, heads_ref, kept_ref, given_ref):
    c, z = place_ref[0], place_ref[1]
    for i in range(len(FAR[0])):
        kept_ref[i] = heads_ref[head_of(i, c, z, FAR)]
        given_ref[i] = heads_ref[head_of(i, 1 - c, z, FAR)]


SMEM = pl.BlockSpec(memory_space=pltpu.SMEM)
VMEM = pl.BlockSpec(memory_space=pltpu.VMEM)


def deal(place, heads, interpret=False):
    shape = jax.ShapeDtypeStruct((len(FAR[0]), 8, ENC), jnp.bfloat16)
    return pl.pallas_call(
        deal_body, out_shape=[shape, shape], in_specs=[SMEM, VMEM], out_specs=[VMEM] * 2, interpret=interpret, name="deal"
    )(place, heads)


def gather_body(place_ref, near_ref, far_ref, out_ref):
    c, z = place_ref[0], place_ref[1]
    for ref, offsets in ((near_ref, NEAR), (far_ref, FAR)):
        for i in range(len(offsets[0])):
            out_ref[head_of(i, c, z, offsets)] = jnp.sum(ref[:, i].astype(jnp.float32), axis=0).astype(jnp.bfloat16)


def gather(place, near, far, interpret=False):
    shape = jax.ShapeDtypeStruct((HEADS, 8, ENC), jnp.bfloat16)
    return pl.pallas_call(
        gather_body, out_shape=shape, in_specs=[SMEM, VMEM, VMEM], out_specs=VMEM, interpret=interpret, name="gather"
    )(place, near, far)


def swap(array):
    return lax.ppermute(array, "c", [(0, 1), (1, 0)])


def exchange(array, axis):
    return lax.all_to_all(array, axis, split_axis=0, concat_axis=0, tiled=True)


def spread(array, axis, count):
    return exchange(jnp.broadcast_to(array[None], (count,) + array.shape), axis)


def total(array):
    return array.astype(jnp.float32).sum(0)


def fetch(array, turns):
    pairs = []
    for c in range(2):
        for z in range(HEADS):
            turn = turns[(c + z) % 2 * (1 + c)]
            core = 1 - c if (turn % 2 == 0) == (turns[0] != 0) else c
            pairs.append((core * HEADS + (z + turn) % HEADS, c * HEADS + z))
    assert len({source for source, _ in pairs}) == len(pairs)
    return lax.ppermute(array, ("c", "z"), pairs)


def local(queries, w_kv, encodings, counts, owner_rank, owner_span, grad_ctx):
    c = lax.axis_index("c")
    z = lax.axis_index("z")
    place = jnp.stack([c, z]).astype(jnp.int32)
    plane = lax.axis_index("y") * 4 + lax.axis_index("x")
    piece = lax.dynamic_slice(w_kv, (c, plane * 8, 0), (1, 8, ENC))[0]
    heads = spread(piece, "z", HEADS)
    kept, given = deal(place, heads)
    mine = jnp.stack([kept, swap(given)])
    near = []
    for turns in zip(*NEAR):
        near.append(fetch(w_kv, turns))

    packed = pack(counts, owner_rank, owner_span, encodings)
    arrived = exchange(packed.reshape(PLANE, 2 * CAP, EXT), ("y", "x")).reshape(ROWS, EXT)
    other = swap(arrived)
    weights = spread(mine, ("y", "x"), PLANE)
    tokens = (queries, grad_ctx, swap(queries), swap(grad_ctx))

    gq, gq2, part, rows, mask = attend_near(place, arrived, other, tokens, near)
    near_part = exchange(part, ("y", "x"))
    gq, gq2, part = attend_far(place, rows, mask, tokens, weights, gq, gq2)
    far_part = exchange(part, ("y", "x"))

    sums = gather(place, near_part, far_part)
    final = (total(exchange(sums, "z")) / DP).astype(jnp.bfloat16)
    block = spread(final, ("y", "x"), PLANE).reshape(HEAD_DIM, ENC)
    grad_value = jnp.where(z % 2 == c, block, swap(block))
    own_head = (lax.broadcasted_iota(jnp.int32, gq.shape, 1) // HEAD_DIM) % 2 == c
    return jnp.where(own_head, gq, swap(gq2)), grad_value


def solution(mesh):
    fine = Mesh(mesh.devices.reshape(4, 4, 2, HEADS), ("y", "x", "c", "z"))
    every = ("y", "x", "c", "z")
    in_specs = (
        P(every, None),
        P(None, "z", None),
        P(every, None),
        P(every),
        P(every),
        P(every),
        P(every, None),
    )
    out_specs = (P(every, None), P("z", None))
    return jax.shard_map(local, mesh=fine, in_specs=in_specs, out_specs=out_specs, check_vma=False)
```

```python
import jax
import jax.numpy as jnp
from jax import lax
from jax.experimental import pallas as pl
from jax.experimental.pallas import tpu as pltpu
from jax.sharding import Mesh
from jax.sharding import PartitionSpec as P

HEADS = 16
HEAD_DIM = 128
SPAN = 64
ENC = 896
TOK = 256
ROWS = 384
DP = 32
CAP = 12
PLANE = 16
EXT = ENC + 128
BIG = 2.0**100
SCALE = 1.0 / HEAD_DIM**0.5
LOG2E = 1.4426950408889634


NN = (((1,), (0,)), ((), ()))
NT = (((1,), (1,)), ((), ()))
TN = (((0,), (0,)), ((), ()))


def dot(a, b, dims):
    return lax.dot_general(a, b, dims, preferred_element_type=jnp.float32)


def pack_body(count_ref, rank_ref, span_ref, enc_ref, out_ref):
    rank = rank_ref[...].reshape(1, ROWS)
    live = lax.broadcasted_iota(jnp.int32, (1, ROWS), 1) < count_ref[0]
    owner = lax.broadcasted_iota(jnp.int32, (DP, ROWS), 0)
    hit = ((owner == rank) & live).astype(jnp.float32)
    earlier = lax.broadcasted_iota(jnp.int32, (ROWS, ROWS), 0) < lax.broadcasted_iota(jnp.int32, (ROWS, ROWS), 1)
    before = dot(hit.astype(jnp.bfloat16), earlier.astype(jnp.float32).astype(jnp.bfloat16), NN)
    slot = jnp.sum(before * hit, axis=0, keepdims=True).astype(jnp.int32)
    target = jnp.where(live, rank * CAP + slot, -1)
    place = (lax.broadcasted_iota(jnp.int32, (ROWS, ROWS), 0) == target).astype(jnp.float32).astype(jnp.bfloat16)
    spans = (lax.broadcasted_iota(jnp.int32, (128, ROWS), 0) == span_ref[...].reshape(1, ROWS)).astype(jnp.float32).astype(jnp.bfloat16)
    out_ref[:, :ENC] = dot(place, enc_ref[...], NN).astype(jnp.bfloat16)
    out_ref[:, ENC:] = dot(place, spans, NT).astype(jnp.bfloat16)


def pack(counts, rank, span, enc, interpret=False):
    vmem = pl.BlockSpec(memory_space=pltpu.VMEM)
    return pl.pallas_call(
        pack_body,
        out_shape=jax.ShapeDtypeStruct((ROWS, EXT), jnp.bfloat16),
        in_specs=[pl.BlockSpec(memory_space=pltpu.SMEM), vmem, vmem, vmem],
        out_specs=vmem,
        interpret=interpret,
        name="pack",
    )(counts, rank, span, enc)


NEAR = ((2, -2, 0), (1, -1, 3), (1, -1, -3))
FAR = ((4, -4, 6, -6, 8), (-3, 5, -5, 7, -7), (3, 5, -5, 7, -7))


def choose(i, options):
    if isinstance(i, int):
        return options[i]
    result = options[-1]
    for k in range(len(options) - 2, -1, -1):
        result = jnp.where(i == k, options[k], result)
    return result


def head_of(i, place, offsets, other=False):
    c, z = place[0] >> 4, place[0] & (HEADS - 1)
    if other:
        c = 1 - c
    even, first, second = (choose(i, row) for row in offsets)
    turn = jnp.where((c + z) & 1 == 0, even, jnp.where(c == 0, first, second))
    return (z + turn) & (HEADS - 1)


def attend_step(rows_ref, mask_ref, q_ref, g_ref, q2_ref, g2_ref, w_ref, gq_ref, gq2_ref, part_ref, dval_ref):
    step = pl.program_id(0)
    group = part_ref.shape[1]
    rows = rows_ref[...]
    pair = dot(rows, w_ref[...], NT).astype(jnp.bfloat16)
    token = lax.broadcasted_iota(jnp.int32, (TOK, 128), 0)
    spans = (lax.broadcasted_iota(jnp.int32, (TOK, 128), 1) == token // SPAN).astype(jnp.float32).astype(jnp.bfloat16)
    spots = []
    for k, (q_ref_, g_ref_, out_ref) in enumerate(((q_ref, g_ref, gq_ref), (q2_ref, g2_ref, gq2_ref))):
        at = slice(k * ROWS, (k + 1) * ROWS)
        key, value, g = pair[at, :HEAD_DIM], pair[at, HEAD_DIM:], g_ref_[...]
        scores = dot(jnp.concatenate([q_ref_[...], spans], 1), jnp.concatenate([key, mask_ref[at, :]], 1), NT)
        spots.append((at, key, g, scores, dot(g, value, NT), out_ref))
    for at, key, g, scores, dprob, out_ref in spots:
        highest = jnp.max(scores, axis=1, keepdims=True)
        weights = jnp.exp2((scores - highest) * (SCALE * LOG2E))
        probs = weights * (1.0 / jnp.sum(weights, axis=1, keepdims=True))
        low = probs.astype(jnp.bfloat16)
        delta = jnp.sum(low.astype(jnp.float32) * dprob, axis=1, keepdims=True)
        dscore = (probs * (dprob - delta)).astype(jnp.bfloat16)
        out_ref[...] = (dot(dscore, key, NN) * SCALE).astype(jnp.bfloat16)
        turned = dot(g, low, TN).astype(jnp.bfloat16)
        dval_ref[pl.ds(pl.multiple_of(step * HEAD_DIM, HEAD_DIM), HEAD_DIM), at] = turned

    @pl.when(step == group - 1)
    def _():
        partial = dot(dval_ref[...], rows, NN)
        for j in range(group):
            block = partial[j * HEAD_DIM : (j + 1) * HEAD_DIM]
            part_ref[:, j, :, :] = block.reshape(PLANE, 8, ENC).astype(jnp.bfloat16)


def near_body(
    place_ref, own_ref, other_ref, q_ref, g_ref, q2_ref, g2_ref, w0_ref, w1_ref, w2_ref,
    gq_ref, gq2_ref, part_ref, rows_ref, mask_ref, w_ref, dval_ref,
):
    step = pl.program_id(0)

    @pl.when(step == 0)
    def _():
        row = lax.broadcasted_iota(jnp.int32, (ROWS, ROWS), 0)
        col = lax.broadcasted_iota(jnp.int32, (ROWS, ROWS), 1)
        second = row // (ROWS // 2)
        rest = row - second * (ROWS // 2)
        chip = rest // CAP
        owner = jnp.where(place_ref[0] < HEADS, second, 1 - second)
        source = chip * (2 * CAP) + owner * CAP + (rest - chip * CAP)
        select = (source == col).astype(jnp.float32).astype(jnp.bfloat16)
        lane = lax.broadcasted_iota(jnp.int32, (ROWS // 2, 128), 1)
        for k, ref in enumerate((own_ref, other_ref)):
            moved = dot(select, ref[...], NN)
            for p in range(2):
                part = moved[p * (ROWS // 2) : (p + 1) * (ROWS // 2)]
                at = pl.ds(p * ROWS + k * (ROWS // 2), ROWS // 2)
                rows_ref[at, :] = part[:, :ENC].astype(jnp.bfloat16)
                mask_ref[at, :] = jnp.where(lane < 4, (part[:, ENC:] - 1.0) * BIG, 0.0).astype(jnp.bfloat16)

    for j, ref in enumerate((w0_ref, w1_ref, w2_ref)):

        @pl.when(step == j)
        def _(ref=ref):
            w_ref[...] = ref[...].reshape(2 * HEAD_DIM, ENC)

    attend_step(rows_ref, mask_ref, q_ref, g_ref, q2_ref, g2_ref, w_ref, gq_ref, gq2_ref, part_ref, dval_ref)


def far_body(
    place_ref, rows_ref, mask_ref, q_ref, g_ref, q2_ref, g2_ref, wk_ref, wv_ref, a0, a1,
    gq_ref, gq2_ref, part_ref, w_ref, dval_ref,
):
    w_ref[:HEAD_DIM, :] = wk_ref[...].reshape(HEAD_DIM, ENC)
    w_ref[HEAD_DIM:, :] = wv_ref[...].reshape(HEAD_DIM, ENC)
    attend_step(rows_ref, mask_ref, q_ref, g_ref, q2_ref, g2_ref, w_ref, gq_ref, gq2_ref, part_ref, dval_ref)


WIDE = jax.ShapeDtypeStruct((TOK, HEADS * HEAD_DIM), jnp.bfloat16)


def whole(*shape):
    return pl.BlockSpec(shape, lambda i, place: (0,) * len(shape))


def head_block(offsets):
    return pl.BlockSpec((TOK, HEAD_DIM), lambda i, place: (0, head_of(i, place, offsets)))


def part_of(group):
    return jax.ShapeDtypeStruct((PLANE, group, 8, ENC), jnp.bfloat16)


def work(group):
    return [pltpu.VMEM((2 * HEAD_DIM, ENC), jnp.bfloat16), pltpu.VMEM((group * HEAD_DIM, 2 * ROWS), jnp.bfloat16)]


def attend_near(place, own, other, tokens, weights, interpret=False):
    head = head_block(NEAR)
    group = len(weights)
    return pl.pallas_call(
        near_body,
        grid_spec=pltpu.PrefetchScalarGridSpec(
            num_scalar_prefetch=1,
            grid=(group,),
            in_specs=[whole(ROWS, EXT)] * 2 + [head] * 4 + [whole(2, HEAD_DIM, ENC)] * group,
            out_specs=[head, head, whole(PLANE, group, 8, ENC), whole(2 * ROWS, ENC), whole(2 * ROWS, 128)],
            scratch_shapes=work(group),
        ),
        out_shape=[
            WIDE,
            WIDE,
            part_of(group),
            jax.ShapeDtypeStruct((2 * ROWS, ENC), jnp.bfloat16),
            jax.ShapeDtypeStruct((2 * ROWS, 128), jnp.bfloat16),
        ],
        interpret=interpret,
        name="near",
    )(place, own, other, *tokens, *weights)


def attend_far(place, rows, mask, tokens, weights, gq, gq2, interpret=False):
    head = head_block(FAR)
    group = weights.shape[2]
    kv = lambda pick: pl.BlockSpec((PLANE, 1, 1, 8, ENC), lambda i, place: (0, pick(place[0] >> 4), i, 0, 0))
    kept = pl.BlockSpec(memory_space=pl.ANY)
    return pl.pallas_call(
        far_body,
        grid_spec=pltpu.PrefetchScalarGridSpec(
            num_scalar_prefetch=1,
            grid=(group,),
            in_specs=[whole(2 * ROWS, ENC), whole(2 * ROWS, 128)]
            + [head] * 4
            + [kv(lambda c: c), kv(lambda c: 1 - c)]
            + [kept] * 2,
            out_specs=[head, head, whole(PLANE, group, 8, ENC)],
            scratch_shapes=work(group),
        ),
        out_shape=[WIDE, WIDE, part_of(group)],
        input_output_aliases={9: 0, 10: 1},
        interpret=interpret,
        name="far",
    )(place, rows, mask, *tokens, weights, weights, gq, gq2)


def deal_body(place_ref, heads_ref, kept_ref, given_ref):
    for i in range(len(FAR[0])):
        kept_ref[i] = heads_ref[head_of(i, place_ref, FAR)]
        given_ref[i] = heads_ref[head_of(i, place_ref, FAR, True)]


SMEM = pl.BlockSpec(memory_space=pltpu.SMEM)
VMEM = pl.BlockSpec(memory_space=pltpu.VMEM)


def deal(place, heads, interpret=False):
    shape = jax.ShapeDtypeStruct((len(FAR[0]), 8, ENC), jnp.bfloat16)
    return pl.pallas_call(
        deal_body, out_shape=[shape, shape], in_specs=[SMEM, VMEM], out_specs=[VMEM] * 2, interpret=interpret, name="deal"
    )(place, heads)


def arrange_body(place_ref, near_ref, far_ref, out_ref):
    for ref, offsets in ((near_ref, NEAR), (far_ref, FAR)):
        for i in range(len(offsets[0])):
            out_ref[head_of(i, place_ref, offsets)] = ref[i]


def arrange(place, near, far, interpret=False):
    shape = jax.ShapeDtypeStruct((HEADS, 8, ENC), jnp.bfloat16)
    return pl.pallas_call(
        arrange_body, out_shape=shape, in_specs=[SMEM, VMEM, VMEM], out_specs=VMEM, interpret=interpret, name="arrange"
    )(place, near, far)


def swap(array):
    return lax.ppermute(array, "c", [(0, 1), (1, 0)])


def exchange(array, axis):
    return lax.all_to_all(array, axis, split_axis=0, concat_axis=0, tiled=True)


def spread(array, axis, count):
    return exchange(jnp.broadcast_to(array[None], (count,) + array.shape), axis)


def total(array):
    return array.astype(jnp.float32).sum(0)


def fetch(array, turns):
    pairs = []
    for c in range(2):
        for z in range(HEADS):
            turn = turns[(c + z) % 2 * (1 + c)]
            core = 1 - c if (turn % 2 == 0) == (turns[0] != 0) else c
            pairs.append((core * HEADS + (z + turn) % HEADS, c * HEADS + z))
    assert len({source for source, _ in pairs}) == len(pairs)
    return lax.ppermute(array, ("c", "z"), pairs)


def local(queries, w_kv, encodings, counts, owner_rank, owner_span, grad_ctx):
    c = lax.axis_index("c")
    z = lax.axis_index("z")
    place = lax.axis_index(("c", "z")).astype(jnp.int32).reshape(1)
    plane = lax.axis_index("y") * 4 + lax.axis_index("x")
    piece = lax.dynamic_slice(w_kv, (c, plane * 8, 0), (1, 8, ENC))[0]
    heads = spread(piece, "z", HEADS)
    kept, given = deal(place, heads)
    mine = jnp.stack([kept, swap(given)])
    near = []
    for turns in zip(*NEAR):
        near.append(fetch(w_kv, turns))

    packed = pack(counts, owner_rank, owner_span, encodings)
    arrived = exchange(packed.reshape(PLANE, 2 * CAP, EXT), ("y", "x")).reshape(ROWS, EXT)
    other = swap(arrived)
    weights = spread(mine, ("y", "x"), PLANE)
    tokens = (queries, grad_ctx, swap(queries), swap(grad_ctx))

    gq, gq2, part, rows, mask = attend_near(place, arrived, other, tokens, near)
    near_part = exchange(part, ("y", "x"))
    gq, gq2, part = attend_far(place, rows, mask, tokens, weights, gq, gq2)
    far_part = exchange(part, ("y", "x"))

    sums = arrange(place, *(total(part).astype(jnp.bfloat16) for part in (near_part, far_part)))
    final = (total(exchange(sums, "z")) / DP).astype(jnp.bfloat16)
    own_head = (lax.broadcasted_iota(jnp.int32, gq.shape, 1) // HEAD_DIM) % 2 == c
    grad_queries, final = lax.optimization_barrier((jnp.where(own_head, gq, swap(gq2)), final))
    blocks = spread(final, ("y", "x", "c"), DP).reshape(PLANE, 2, 8, ENC)
    return grad_queries, lax.dynamic_index_in_dim(blocks, z % 2, 1, False).reshape(HEAD_DIM, ENC)


def solution(mesh):
    fine = Mesh(mesh.devices.reshape(4, 4, 2, HEADS), ("y", "x", "c", "z"))
    every = ("y", "x", "c", "z")
    in_specs = (
        P(every, None),
        P(None, "z", None),
        P(every, None),
        P(every),
        P(every),
        P(every),
        P(every, None),
    )
    out_specs = (P(every, None), P("z", None))
    return jax.shard_map(local, mesh=fine, in_specs=in_specs, out_specs=out_specs, check_vma=False)
```

```python
import jax
import jax.numpy as jnp
from jax import lax
from jax.experimental import pallas as pl
from jax.experimental.pallas import tpu as pltpu
from jax.sharding import Mesh
from jax.sharding import PartitionSpec as P

HEADS = 16
HEAD_DIM = 128
SPAN = 64
ENC = 896
TOK = 256
ROWS = 384
DP = 32
CAP = 12
PLANE = 16
HALF = HEADS // 2
EXT = ENC + 128
BIG = 2.0**100
SCALE = 1.0 / HEAD_DIM**0.5
LOG2E = 1.4426950408889634


NN = (((1,), (0,)), ((), ()))
NT = (((1,), (1,)), ((), ()))
TN = (((0,), (0,)), ((), ()))


def dot(a, b, dims):
    return lax.dot_general(a, b, dims, preferred_element_type=jnp.float32)


def pack_body(count_ref, rank_ref, span_ref, enc_ref, out_ref):
    rank = rank_ref[...].reshape(1, ROWS)
    live = lax.broadcasted_iota(jnp.int32, (1, ROWS), 1) < count_ref[0]
    owner = lax.broadcasted_iota(jnp.int32, (DP, ROWS), 0)
    hit = ((owner == rank) & live).astype(jnp.float32)
    earlier = lax.broadcasted_iota(jnp.int32, (ROWS, ROWS), 0) < lax.broadcasted_iota(jnp.int32, (ROWS, ROWS), 1)
    before = dot(hit.astype(jnp.bfloat16), earlier.astype(jnp.float32).astype(jnp.bfloat16), NN)
    slot = jnp.sum(before * hit, axis=0, keepdims=True).astype(jnp.int32)
    target = jnp.where(live, rank * CAP + slot, -1)
    place = (lax.broadcasted_iota(jnp.int32, (ROWS, ROWS), 0) == target).astype(jnp.float32).astype(jnp.bfloat16)
    spans = (lax.broadcasted_iota(jnp.int32, (128, ROWS), 0) == span_ref[...].reshape(1, ROWS)).astype(jnp.float32).astype(jnp.bfloat16)
    out_ref[:, :ENC] = dot(place, enc_ref[...], NN).astype(jnp.bfloat16)
    out_ref[:, ENC:] = dot(place, spans, NT).astype(jnp.bfloat16)


def pack(counts, rank, span, enc, interpret=False):
    vmem = pl.BlockSpec(memory_space=pltpu.VMEM)
    return pl.pallas_call(
        pack_body,
        out_shape=jax.ShapeDtypeStruct((ROWS, EXT), jnp.bfloat16),
        in_specs=[pl.BlockSpec(memory_space=pltpu.SMEM), vmem, vmem, vmem],
        out_specs=vmem,
        interpret=interpret,
        name="pack",
    )(counts, rank, span, enc)


NEAR = ((2, -2, 0), (1, -1, 3), (1, -1, -3))
FAR = ((4, -4, 6, -6, 8), (-3, 5, -5, 7, -7), (3, 5, -5, 7, -7))


def choose(i, options):
    if isinstance(i, int):
        return options[i]
    result = options[-1]
    for k in range(len(options) - 2, -1, -1):
        result = jnp.where(i == k, options[k], result)
    return result


def head_of(i, place, offsets, other=False):
    c, z = place[0] >> 4, place[0] & (HEADS - 1)
    if other:
        c = 1 - c
    even, first, second = (choose(i, row) for row in offsets)
    turn = jnp.where((c + z) & 1 == 0, even, jnp.where(c == 0, first, second))
    return (z + turn) & (HEADS - 1)


def attend_step(rows_ref, mask_ref, q_ref, g_ref, q2_ref, g2_ref, w_ref, gq_ref, gq2_ref, part_ref, dval_ref, first=0):
    step = pl.program_id(0)
    group = part_ref.shape[1] - first
    rows = rows_ref[...]
    pair = dot(rows, w_ref[...], NT).astype(jnp.bfloat16)
    token = lax.broadcasted_iota(jnp.int32, (TOK, 128), 0)
    spans = (lax.broadcasted_iota(jnp.int32, (TOK, 128), 1) == token // SPAN).astype(jnp.float32).astype(jnp.bfloat16)
    spots = []
    for k, (q_ref_, g_ref_, out_ref) in enumerate(((q_ref, g_ref, gq_ref), (q2_ref, g2_ref, gq2_ref))):
        at = slice(k * ROWS, (k + 1) * ROWS)
        key, value, g = pair[at, :HEAD_DIM], pair[at, HEAD_DIM:], g_ref_[...]
        scores = dot(jnp.concatenate([q_ref_[...], spans], 1), jnp.concatenate([key, mask_ref[at, :]], 1), NT)
        spots.append((at, key, g, scores, dot(g, value, NT), out_ref))
    for at, key, g, scores, dprob, out_ref in spots:
        highest = jnp.max(scores, axis=1, keepdims=True)
        weights = jnp.exp2((scores - highest) * (SCALE * LOG2E))
        probs = weights * (1.0 / jnp.sum(weights, axis=1, keepdims=True))
        low = probs.astype(jnp.bfloat16)
        delta = jnp.sum(low.astype(jnp.float32) * dprob, axis=1, keepdims=True)
        dscore = (probs * (dprob - delta)).astype(jnp.bfloat16)
        out_ref[...] = (dot(dscore, key, NN) * SCALE).astype(jnp.bfloat16)
        turned = dot(g, low, TN).astype(jnp.bfloat16)
        dval_ref[pl.ds(pl.multiple_of(step * HEAD_DIM, HEAD_DIM), HEAD_DIM), at] = turned

    @pl.when(step == group - 1)
    def _():
        partial = dot(dval_ref[...], rows, NN)
        for j in range(group):
            block = partial[j * HEAD_DIM : (j + 1) * HEAD_DIM]
            part_ref[:, first + j, :, :] = block.reshape(PLANE, 8, ENC).astype(jnp.bfloat16)


def near_body(
    place_ref, own_ref, other_ref, q_ref, g_ref, q2_ref, g2_ref, w0_ref, w1_ref, w2_ref,
    gq_ref, gq2_ref, part_ref, rows_ref, mask_ref, w_ref, dval_ref,
):
    step = pl.program_id(0)

    @pl.when(step == 0)
    def _():
        row = lax.broadcasted_iota(jnp.int32, (ROWS, ROWS), 0)
        col = lax.broadcasted_iota(jnp.int32, (ROWS, ROWS), 1)
        second = row // (ROWS // 2)
        rest = row - second * (ROWS // 2)
        chip = rest // CAP
        owner = jnp.where(place_ref[0] < HEADS, second, 1 - second)
        source = chip * (2 * CAP) + owner * CAP + (rest - chip * CAP)
        select = (source == col).astype(jnp.float32).astype(jnp.bfloat16)
        lane = lax.broadcasted_iota(jnp.int32, (ROWS // 2, 128), 1)
        for k, ref in enumerate((own_ref, other_ref)):
            moved = dot(select, ref[...], NN)
            for p in range(2):
                part = moved[p * (ROWS // 2) : (p + 1) * (ROWS // 2)]
                at = pl.ds(p * ROWS + k * (ROWS // 2), ROWS // 2)
                rows_ref[at, :] = part[:, :ENC].astype(jnp.bfloat16)
                mask_ref[at, :] = jnp.where(lane < 4, (part[:, ENC:] - 1.0) * BIG, 0.0).astype(jnp.bfloat16)

    for j, ref in enumerate((w0_ref, w1_ref, w2_ref)):

        @pl.when(step == j)
        def _(ref=ref):
            w_ref[...] = ref[...].reshape(2 * HEAD_DIM, ENC)

    attend_step(rows_ref, mask_ref, q_ref, g_ref, q2_ref, g2_ref, w_ref, gq_ref, gq2_ref, part_ref, dval_ref)


def far_body(
    place_ref, rows_ref, mask_ref, q_ref, g_ref, q2_ref, g2_ref, wk_ref, wv_ref, near_ref, a0, a1,
    gq_ref, gq2_ref, part_ref, w_ref, dval_ref,
):
    w_ref[:HEAD_DIM, :] = wk_ref[...].reshape(HEAD_DIM, ENC)
    w_ref[HEAD_DIM:, :] = wv_ref[...].reshape(HEAD_DIM, ENC)
    first = near_ref.shape[1]
    attend_step(rows_ref, mask_ref, q_ref, g_ref, q2_ref, g2_ref, w_ref, gq_ref, gq2_ref, part_ref, dval_ref, first)

    @pl.when(pl.program_id(0) == 0)
    def _():
        part_ref[:, :first] = near_ref[...]


WIDE = jax.ShapeDtypeStruct((TOK, HEADS * HEAD_DIM), jnp.bfloat16)


def whole(*shape):
    return pl.BlockSpec(shape, lambda i, place: (0,) * len(shape))


def head_block(offsets):
    return pl.BlockSpec((TOK, HEAD_DIM), lambda i, place: (0, head_of(i, place, offsets)))


def part_of(group):
    return jax.ShapeDtypeStruct((PLANE, group, 8, ENC), jnp.bfloat16)


def work(group):
    return [pltpu.VMEM((2 * HEAD_DIM, ENC), jnp.bfloat16), pltpu.VMEM((group * HEAD_DIM, 2 * ROWS), jnp.bfloat16)]


def attend_near(place, own, other, tokens, weights, interpret=False):
    head = head_block(NEAR)
    group = len(weights)
    return pl.pallas_call(
        near_body,
        grid_spec=pltpu.PrefetchScalarGridSpec(
            num_scalar_prefetch=1,
            grid=(group,),
            in_specs=[whole(ROWS, EXT)] * 2 + [head] * 4 + [whole(2, HEAD_DIM, ENC)] * group,
            out_specs=[head, head, whole(PLANE, group, 8, ENC), whole(2 * ROWS, ENC), whole(2 * ROWS, 128)],
            scratch_shapes=work(group),
        ),
        out_shape=[
            WIDE,
            WIDE,
            part_of(group),
            jax.ShapeDtypeStruct((2 * ROWS, ENC), jnp.bfloat16),
            jax.ShapeDtypeStruct((2 * ROWS, 128), jnp.bfloat16),
        ],
        interpret=interpret,
        name="near",
    )(place, own, other, *tokens, *weights)


def attend_far(place, rows, mask, tokens, weights, near, gq, gq2, interpret=False):
    head = head_block(FAR)
    group = weights.shape[2]
    kv = lambda pick: pl.BlockSpec((PLANE, 1, 1, 8, ENC), lambda i, place: (0, pick(place[0] >> 4), i, 0, 0))
    kept = pl.BlockSpec(memory_space=pl.ANY)
    return pl.pallas_call(
        far_body,
        grid_spec=pltpu.PrefetchScalarGridSpec(
            num_scalar_prefetch=1,
            grid=(group,),
            in_specs=[whole(2 * ROWS, ENC), whole(2 * ROWS, 128)]
            + [head] * 4
            + [kv(lambda c: c), kv(lambda c: 1 - c)]
            + [whole(*near.shape)]
            + [kept] * 2,
            out_specs=[head, head, whole(PLANE, HALF, 8, ENC)],
            scratch_shapes=work(group),
        ),
        out_shape=[WIDE, WIDE, part_of(HALF)],
        input_output_aliases={10: 0, 11: 1},
        interpret=interpret,
        name="far",
    )(place, rows, mask, *tokens, weights, weights, near, gq, gq2)


def deal_body(place_ref, heads_ref, kept_ref, given_ref):
    for i in range(len(FAR[0])):
        kept_ref[i] = heads_ref[head_of(i, place_ref, FAR)]
        given_ref[i] = heads_ref[head_of(i, place_ref, FAR, True)]


SMEM = pl.BlockSpec(memory_space=pltpu.SMEM)
VMEM = pl.BlockSpec(memory_space=pltpu.VMEM)


def deal(place, heads, interpret=False):
    shape = jax.ShapeDtypeStruct((len(FAR[0]), 8, ENC), jnp.bfloat16)
    return pl.pallas_call(
        deal_body, out_shape=[shape, shape], in_specs=[SMEM, VMEM], out_specs=[VMEM] * 2, interpret=interpret, name="deal"
    )(place, heads)


def arrange_body(place_ref, sums_ref, out_ref):
    both = tuple(n + f for n, f in zip(NEAR, FAR))
    for i in range(HALF):
        out_ref[head_of(i, place_ref, both)] = sums_ref[i]


def arrange(place, sums, interpret=False):
    shape = jax.ShapeDtypeStruct((HEADS, 8, ENC), jnp.bfloat16)
    return pl.pallas_call(
        arrange_body, out_shape=shape, in_specs=[SMEM, VMEM], out_specs=VMEM, interpret=interpret, name="arrange"
    )(place, sums)


def swap(array):
    return lax.ppermute(array, "c", [(0, 1), (1, 0)])


def exchange(array, axis):
    return lax.all_to_all(array, axis, split_axis=0, concat_axis=0, tiled=True)


def spread(array, axis, count):
    return exchange(jnp.broadcast_to(array[None], (count,) + array.shape), axis)


def total(array):
    return array.astype(jnp.float32).sum(0)


def fetch(array, turns):
    pairs = []
    for c in range(2):
        for z in range(HEADS):
            turn = turns[(c + z) % 2 * (1 + c)]
            core = 1 - c if (turn % 2 == 0) == (turns[0] != 0) else c
            pairs.append((core * HEADS + (z + turn) % HEADS, c * HEADS + z))
    assert len({source for source, _ in pairs}) == len(pairs)
    return lax.ppermute(array, ("c", "z"), pairs)


def local(queries, w_kv, encodings, counts, owner_rank, owner_span, grad_ctx):
    c = lax.axis_index("c")
    z = lax.axis_index("z")
    place = lax.axis_index(("c", "z")).astype(jnp.int32).reshape(1)
    plane = lax.axis_index("y") * 4 + lax.axis_index("x")
    piece = lax.dynamic_slice(w_kv, (c, plane * 8, 0), (1, 8, ENC))[0]
    heads = spread(piece, "z", HEADS)
    kept, given = deal(place, heads)
    mine = jnp.stack([kept, swap(given)])
    near = []
    for turns in zip(*NEAR):
        near.append(fetch(w_kv, turns))

    packed = pack(counts, owner_rank, owner_span, encodings)
    arrived = exchange(packed.reshape(PLANE, 2 * CAP, EXT), ("y", "x")).reshape(ROWS, EXT)
    other = swap(arrived)
    weights = spread(mine, ("y", "x"), PLANE)
    tokens = (queries, grad_ctx, swap(queries), swap(grad_ctx))

    gq, gq2, part, rows, mask = attend_near(place, arrived, other, tokens, near)
    gq, gq2, part = attend_far(place, rows, mask, tokens, weights, part, gq, gq2)
    sums = arrange(place, total(exchange(part, ("y", "x"))).astype(jnp.bfloat16))
    final = (total(exchange(sums, "z")) / DP).astype(jnp.bfloat16)
    own_head = (lax.broadcasted_iota(jnp.int32, gq.shape, 1) // HEAD_DIM) % 2 == c
    grad_queries, final = lax.optimization_barrier((jnp.where(own_head, gq, swap(gq2)), final))
    blocks = spread(final, ("y", "x", "c"), DP).reshape(PLANE, 2, 8, ENC)
    return grad_queries, lax.dynamic_index_in_dim(blocks, z % 2, 1, False).reshape(HEAD_DIM, ENC)


def solution(mesh):
    fine = Mesh(mesh.devices.reshape(4, 4, 2, HEADS), ("y", "x", "c", "z"))
    every = ("y", "x", "c", "z")
    in_specs = (
        P(every, None),
        P(None, "z", None),
        P(every, None),
        P(every),
        P(every),
        P(every),
        P(every, None),
    )
    out_specs = (P(every, None), P("z", None))
    return jax.shard_map(local, mesh=fine, in_specs=in_specs, out_specs=out_specs, check_vma=False)
```
